32 devices in a mesh: space: 4 (over y, core), vel: 8 (over z, x).
Axes of the slice: x: 2, y: 2, z: 4, core: 2. Of those that a mesh axis runs over, the one named last changes fastest.
Arguments:
- distribution: float32 [4, 256, 13824], P('space', None, 'vel'), may hold values from -6 to 6
- neighbours: int32 [4, 4], P('space'), may hold values from -1 to 3, as said below
- block_level: int32 [4], P('space'), may hold values from 0 to 2
- collide_mask: int32 [1024], P('space'), may hold values from 0 to 1, as said below
- gain_first: float32 [6, 13824], replicated, may hold values from -1.8 to 1.8
- gain_second: float32 [6, 13824], replicated, may hold values from -1.8 to 1.8
- loss_rates: float32 [13824], replicated, may hold values from 0.2 to 2
Outputs:
- distribution_next: float32 [4, 256, 13824], P('space', None, 'vel')
The draws below stay inside these ranges and needn't reach their ends.
Inputs may be any that keep to these rules, and one draw needn't show every extreme that they name: `neighbours`: each entry is -1 or a block held by the same index of space as the block itself or by the index one below or one above (index s holds blocks s * 1 to (s + 1) - 1). `collide_mask`: the cells of one index of space (its 1 block) hold at most 128 ones, and some index holds exactly 128.
All inputs are finite; a program needn't handle non-finite values.
Results may differ from the reference program's by a relative error of at most 0.0003.
Values sent between devices are 32-bit elements; how exact they have to be, the bound alone decides.
A program may use at most 128 MiB of HBM per device.

```python
import math
import jax
import jax.numpy as jnp
from jax import lax

BSIDE = 16
VDIM = 24
TERMS = 6
LEVELS = 3
BLK_DEV = 1
NB = 4
ACT = 128
NV = 13824


def draw_neighbours(key, part):
    spaces = NB // BLK_DEV
    blocks = jnp.arange(NB, dtype=jnp.int32)
    owner_index = blocks // BLK_DEV
    key_kind, key_within = jax.random.split(jax.random.fold_in(key, 11), 2)
    face_kind = jax.random.randint(key_kind, (NB, 4), 0, 8)
    offset = jnp.where(face_kind <= 2, -1, jnp.where(face_kind <= 5, 0, 1))
    first_block = (blocks % BLK_DEV == 0) & (owner_index > 0)
    final_block = (blocks % BLK_DEV == BLK_DEV - 1) & (owner_index < spaces - 1)
    offset = offset.at[:, 2].set(jnp.where(first_block, -1, offset[:, 2]))
    offset = offset.at[:, 3].set(jnp.where(final_block, 1, offset[:, 3]))
    face_kind = face_kind.at[:, 2].set(jnp.where(first_block, 1, face_kind[:, 2]))
    face_kind = face_kind.at[:, 3].set(jnp.where(final_block, 7, face_kind[:, 3]))
    target = owner_index[:, None] + offset
    within = jax.random.randint(key_within, (NB, 4), 0, BLK_DEV)
    source = target * BLK_DEV + within
    usable = (face_kind != 0) & (target >= 0) & (target < spaces)
    source = jnp.where(usable, source, -1)
    source = source.at[0, 0].set(-1)
    source = source.at[NB - 2, 1].set(NB - 1)
    return source.astype(jnp.int32)


def draw_collide_mask(key, part):
    spaces = NB // BLK_DEV
    per_space = BLK_DEV * BSIDE * BSIDE
    key_count, key_full, key_order = jax.random.split(jax.random.fold_in(key, 23), 3)
    counts = jax.random.randint(key_count, (spaces,), ACT // 2, ACT + 1)
    busiest = jax.random.randint(key_full, (), 0, spaces)
    counts = counts.at[busiest].set(ACT)

    def one_order(single):
        return jax.random.permutation(single, per_space)
    orders = jax.vmap(one_order)(jax.random.split(key_order, spaces))
    return (orders < counts[:, None]).astype(jnp.int32).reshape(-1)


def set_ends(array, rng, least, top_value):
    longest = array.shape.index(max(array.shape))
    spots = []
    for shift in (0, 1):
        where = [jax.random.randint(jax.random.fold_in(rng, axis), (), 0, length) for axis, length in enumerate(array.shape)]
        where[longest] = (where[longest] + shift) % array.shape[longest]
        spots.append(tuple(where))
    return array.at[spots[0]].set(least).at[spots[1]].set(top_value)


def shard_levels(stream_key, shape, cuts, low, largest):
    level, own = 1.0, jax.random.fold_in(stream_key, 6)
    for position, shards_of in cuts:
        steps = jnp.exp(jax.random.uniform(jax.random.fold_in(own, position), (shards_of,), jnp.float32, low / len(cuts), largest / len(cuts)))
        level = level * jnp.repeat(steps, shape[position] // shards_of).reshape([-1 if axis == position else 1 for axis in range(len(shape))])
    return level


def bell_draw(own_key, shape, spread, limit, cuts=(), kind=jnp.bfloat16):
    values = jax.random.normal(own_key, shape, jnp.float32) * spread
    if len(cuts) > 0:
        values = shard_levels(own_key, shape, cuts, -0.22, 0.18) * values
    return jnp.clip(values, min=-limit, max=limit).astype(kind)


def setup_inputs(seed: int = 0) -> dict:
    key_list = jax.random.split(jax.random.key(seed), 8)
    distribution = bell_draw(key_list[0], (NB, BSIDE * BSIDE, NV), 1.0, 6.0, ((0, 4), (2, 8)), jnp.float32)
    neighbours = draw_neighbours(jax.random.fold_in(key_list[7], 71), 0)
    block_level = set_ends(jax.random.randint(key_list[2], (NB,), 0, LEVELS), jax.random.fold_in(key_list[2], 1), 0, LEVELS - 1).astype(jnp.int32)
    collide_mask = draw_collide_mask(jax.random.fold_in(key_list[7], 71), 0)
    gain_first = bell_draw(key_list[4], (TERMS, NV), 0.3, 1.8, (), jnp.float32)
    gain_second = bell_draw(key_list[5], (TERMS, NV), 0.3, 1.8, (), jnp.float32)
    loss_rates = jnp.clip(jnp.exp(jax.random.uniform(key_list[6], (NV,), jnp.float32, math.log(0.2), math.log(2.0))), 0.2, 2.0)
    return dict(distribution=distribution, neighbours=neighbours, block_level=block_level, collide_mask=collide_mask, gain_first=gain_first, gain_second=gain_second, loss_rates=loss_rates)


weno_eps = 1e-06
courant = 0.2

def weno_value(minus_two, minus_one, middle, plus_one, plus_two):
    guess_low = (2.0 * minus_two - 7.0 * minus_one + 11.0 * middle) / 6.0
    guess_mid = (-minus_one + 5.0 * middle + 2.0 * plus_one) / 6.0
    guess_high = (2.0 * middle + 5.0 * plus_one - plus_two) / 6.0
    rough_low = 13.0 / 12.0 * (minus_two - 2.0 * minus_one + middle) ** 2 + 0.25 * (minus_two - 4.0 * minus_one + 3.0 * middle) ** 2
    rough_mid = 13.0 / 12.0 * (minus_one - 2.0 * middle + plus_one) ** 2 + 0.25 * (minus_one - plus_one) ** 2
    rough_high = 13.0 / 12.0 * (middle - 2.0 * plus_one + plus_two) ** 2 + 0.25 * (3.0 * middle - 4.0 * plus_one + plus_two) ** 2
    weight_low = 0.1 / (weno_eps + rough_low) ** 2
    weight_mid = 0.6 / (weno_eps + rough_mid) ** 2
    weight_high = 0.3 / (weno_eps + rough_high) ** 2
    return (weight_low * guess_low + weight_mid * guess_mid + weight_high * guess_high) / (weight_low + weight_mid + weight_high)

def edge_values(padded, along, cell_count):

    def shifted(offset):
        return lax.slice_in_dim(padded, offset, offset + cell_count + 1, axis=along)
    upwind_low = weno_value(shifted(0), shifted(1), shifted(2), shifted(3), shifted(4))
    upwind_high = weno_value(shifted(5), shifted(4), shifted(3), shifted(2), shifted(1))
    return (upwind_low, upwind_high)

def flux_change(padded, along, cell_count, velocity):
    from_low, from_high = edge_values(padded, along, cell_count)
    step_low = lax.slice_in_dim(from_low, 1, cell_count + 1, axis=along) - lax.slice_in_dim(from_low, 0, cell_count, axis=along)
    step_high = lax.slice_in_dim(from_high, 1, cell_count + 1, axis=along) - lax.slice_in_dim(from_high, 0, cell_count, axis=along)
    return jnp.maximum(velocity, 0.0) * step_low + jnp.minimum(velocity, 0.0) * step_high

def transport_rate(padded_first, padded_second, along, cell_count, speed_first, speed_second, courant_ratio):
    change = flux_change(padded_first, along, cell_count, speed_first) + flux_change(padded_second, along + 1, cell_count, speed_second)
    return -courant_ratio * change

def grid_speeds(vel_start, vel_width, vdim):
    index = vel_start + jnp.arange(vel_width, dtype=jnp.int32)
    first_index = index // (vdim * vdim)
    second_index = index // vdim % vdim
    half = (vdim - 1) / 2.0
    return ((first_index.astype(jnp.float32) - half) / half, (second_index.astype(jnp.float32) - half) / half)

def hartley(length):
    grid_index = jnp.arange(length, dtype=jnp.float32)
    angle_table = 2.0 * jnp.pi * grid_index[:, None] * grid_index[None, :] / length
    return (jnp.cos(angle_table) + jnp.sin(angle_table)) / jnp.sqrt(jnp.float32(length))

def hartley_cube(velocity_cube, hartley_table):
    highest = lax.Precision.HIGHEST
    velocity_cube = jnp.einsum('cijk,kl->cijl', velocity_cube, hartley_table, precision=highest)
    velocity_cube = jnp.einsum('cijk,jl->cilk', velocity_cube, hartley_table, precision=highest)
    return jnp.einsum('cijk,il->cljk', velocity_cube, hartley_table, precision=highest)

def collide(cell_rows, gain_first, gain_second, loss_rates, hartley_table):
    row_count = cell_rows.shape[0]
    vdim = hartley_table.shape[0]
    velocity_cube = cell_rows.reshape(row_count, vdim, vdim, vdim)
    spectrum = hartley_cube(velocity_cube, hartley_table)
    gain_total = jnp.zeros_like(velocity_cube)
    for term_index in range(gain_first.shape[0]):
        gain_one = hartley_cube(spectrum * gain_first[term_index].reshape(vdim, vdim, vdim), hartley_table)
        gain_two = hartley_cube(spectrum * gain_second[term_index].reshape(vdim, vdim, vdim), hartley_table)
        gain_total = gain_total + gain_one * gain_two
    loss_part = hartley_cube(spectrum * loss_rates.reshape(vdim, vdim, vdim), hartley_table)
    return (gain_total - velocity_cube * loss_part).reshape(row_count, -1)

def block_rates(density, neighbours, block_level, speed_first, speed_second):
    block_side = density.shape[1]

    def one_block(block_index):
        own_block = density[block_index]
        sources = neighbours[block_index]

        def ghost(face_index):
            source = sources[face_index]
            return density[jnp.maximum(source, 0)] * (source >= 0).astype(jnp.float32)
        ghost_west = ghost(0)[block_side - 3:]
        ghost_east = ghost(1)[:3]
        ghost_south = ghost(2)[:, block_side - 3:]
        ghost_north = ghost(3)[:, :3]
        padded_first = jnp.concatenate([ghost_west, own_block, ghost_east], axis=0)
        padded_second = jnp.concatenate([ghost_south, own_block, ghost_north], axis=1)
        courant_ratio = courant * jnp.exp2(block_level[block_index].astype(jnp.float32))
        return transport_rate(padded_first, padded_second, 0, block_side, speed_first, speed_second, courant_ratio)
    return lax.map(one_block, jnp.arange(NB, dtype=jnp.int32))

def reference(distribution, neighbours, block_level, collide_mask, gain_first, gain_second, loss_rates):
    density = distribution.reshape(NB, BSIDE, BSIDE, NV)
    speed_first, speed_second = grid_speeds(0, NV, VDIM)
    section_one = density + block_rates(density, neighbours, block_level, speed_first, speed_second)
    section_two = 0.5 * density + 0.5 * (section_one + block_rates(section_one, neighbours, block_level, speed_first, speed_second))
    hartley_table = hartley(VDIM)
    flat_cells = section_two.reshape(NB, BSIDE * BSIDE, NV)
    marked = collide_mask.reshape(NB, BSIDE * BSIDE).astype(jnp.float32)

    def collide_block(inputs):
        cell_rows, block_marks = inputs
        return cell_rows + block_marks[:, None] * collide(cell_rows, gain_first, gain_second, loss_rates, hartley_table)
    return lax.map(collide_block, (flat_cells, marked))
```

```python
import functools

import jax
import jax.numpy as jnp
import numpy as np
from jax import lax
from jax.experimental import pallas as pl
from jax.experimental.pallas import tpu as pltpu
from jax.sharding import PartitionSpec as P

BSIDE = 16
VDIM = 24
ACT = 128
LANES = 128
GROUP = 8


weno_eps = 1e-06
courant = 0.2


def speed_rows(vel_start, vel_width):
    index = vel_start + jnp.arange(vel_width, dtype=jnp.int32)
    half = (VDIM - 1) / 2.0
    first = ((index // (VDIM * VDIM)).astype(jnp.float32) - half) / half
    second = ((index // VDIM % VDIM).astype(jnp.float32) - half) / half
    rows = [jnp.abs(first), jnp.abs(second), jnp.where(first < 0, 1.0, 0.0), jnp.where(second < 0, 1.0, 0.0)]
    return jnp.stack(rows + [jnp.zeros_like(first)] * 4)


def pack_kernel(u_ref, pack_ref):
    side = BSIDE
    pack_ref[0 : 3 * side] = u_ref[0 : 3 * side]
    pack_ref[3 * side : 6 * side] = u_ref[(side - 3) * side :]
    for layer in range(3):
        at = (6 + layer) * side
        pack_ref[at : at + side] = u_ref[pl.ds(layer, side, stride=side), :]
        at = (9 + layer) * side
        pack_ref[at : at + side] = u_ref[pl.ds(side - 3 + layer, side, stride=side), :]


def sweep(line, against, speed, flux_ref):
    side = BSIDE

    def oriented(n):
        return jnp.where(against, line(side + 5 - n), line(n))

    values = [oriented(n) for n in range(4)]
    slopes = [values[n + 1] - values[n] for n in range(3)]
    bends = []
    for n in range(2):
        bend = slopes[n + 1] - slopes[n]
        bends.append(bend * bend * (13.0 / 3.0) + 4.0 * weno_eps)
    before = None
    for i in range(side + 1):
        values.append(oriented(i + 4))
        slopes.append(values[i + 4] - values[i + 3])
        bend = slopes[i + 3] - slopes[i + 2]
        bends.append(bend * bend * (13.0 / 3.0) + 4.0 * weno_eps)
        d0, d1, d2, d3 = slopes[i : i + 4]
        tilt_low = 3.0 * d1 - d0
        tilt_mid = d1 + d2
        tilt_high = d3 - 3.0 * d2
        rough_low = bends[i] + tilt_low * tilt_low
        rough_mid = bends[i + 1] + tilt_mid * tilt_mid
        rough_high = bends[i + 2] + tilt_high * tilt_high
        low2 = rough_low * rough_low
        mid2 = rough_mid * rough_mid
        high2 = rough_high * rough_high
        weight_low = mid2 * high2
        low3 = 3.0 * low2
        weight_mid = (low3 + low3) * high2
        weight_high = low3 * mid2
        guess_low = 5.0 * d1 - 2.0 * d0
        guess_mid = d1 + (d2 + d2)
        guess_high = 4.0 * d2 - d3
        above = weight_low * guess_low + weight_mid * guess_mid + weight_high * guess_high
        below = weight_low + weight_mid + weight_high
        edge = values[i + 2] + above / (6.0 * below)
        if before is not None:
            flux_ref[(i - 1) * side : i * side] = speed * (edge - before)
        before = edge


def stage_kernel(final, source_ref, ratio_ref, *refs):
    if final:
        base_ref, u_ref, left_ref, right_ref, speed_ref, out_ref, flux_one, flux_two, flux_turned = refs
    else:
        u_ref, left_ref, right_ref, speed_ref, out_ref, pack_ref, flux_one, flux_two, flux_turned = refs
    side = BSIDE
    lanes = u_ref.shape[1]

    def first_line(n):
        return u_ref[n * side : (n + 1) * side]

    def second_line(n):
        return u_ref[pl.ds(n, side, stride=side), :]

    def ghost(face, strip, layer, own):
        at = (3 * strip + layer) * side
        return (
            source_ref[3 * face] * left_ref[at : at + side]
            + source_ref[3 * face + 1] * own
            + source_ref[3 * face + 2] * right_ref[at : at + side]
        )

    def padded(line, faces, strips):
        ghosts = {}
        for layer in range(3):
            ghosts[layer] = ghost(faces[0], strips[0], layer, line(side - 3 + layer))
            ghosts[side + 3 + layer] = ghost(faces[1], strips[1], layer, line(layer))
        return lambda n: ghosts[n] if n in ghosts else line(n - 3)

    def spread(row):
        return jnp.broadcast_to(speed_ref[row : row + 1], (side, lanes))

    against_first = spread(2) > 0.5
    against_second = spread(3) > 0.5
    sweep(padded(first_line, (0, 1), (1, 0)), against_first, spread(0), flux_one)
    sweep(padded(second_line, (2, 3), (3, 2)), against_second, spread(1), flux_two)
    for n in range(side):
        back = side - 1 - n
        flux_turned[n * side : (n + 1) * side] = jnp.where(
            against_second, flux_two[back * side : (back + 1) * side], flux_two[n * side : (n + 1) * side]
        )
    ratio = ratio_ref[0]
    for n in range(side):
        back = side - 1 - n
        rows = slice(n * side, (n + 1) * side)
        change = jnp.where(against_first, flux_one[back * side : (back + 1) * side], flux_one[rows])
        change = change + flux_turned[pl.ds(n, side, stride=side), :]
        moved = u_ref[rows] - ratio * change
        if final:
            moved = 0.5 * base_ref[rows] + 0.5 * moved
        out_ref[rows] = moved
    if not final:
        pack_kernel(out_ref, pack_ref)


def lane_spec(rows):
    return pl.BlockSpec((rows, LANES), lambda n: (0, n))


def pack(cells):
    count, width = cells.shape
    return pl.pallas_call(
        pack_kernel,
        grid=(pl.cdiv(width, LANES),),
        in_specs=[lane_spec(count)],
        out_specs=lane_spec(12 * BSIDE),
        out_shape=jax.ShapeDtypeStruct((12 * BSIDE, width), jnp.float32),
    )(cells)


def stage(final, source, ratio, arrays):
    count, width = arrays[0].shape
    smem = pl.BlockSpec(memory_space=pltpu.SMEM)
    full = jax.ShapeDtypeStruct((count, width), jnp.float32)
    strips = jax.ShapeDtypeStruct((12 * BSIDE, width), jnp.float32)
    return pl.pallas_call(
        functools.partial(stage_kernel, final),
        grid=(pl.cdiv(width, LANES),),
        in_specs=[smem, smem] + [lane_spec(array.shape[0]) for array in arrays],
        out_specs=lane_spec(count) if final else [lane_spec(count), lane_spec(12 * BSIDE)],
        out_shape=full if final else [full, strips],
        scratch_shapes=[pltpu.VMEM((count, LANES), jnp.float32)] * 3,
    )(source, ratio, *arrays)


def exchange(strips):
    count = lax.axis_size("space")
    up = [(i, i + 1) for i in range(count - 1)]
    return lax.ppermute(strips, "space", up), lax.ppermute(strips, "space", [(j, i) for i, j in up])


def gather_kernel(chosen_ref, cells_ref, out_ref, rows_ref):
    parts, planes, each, plane = out_ref.shape

    def one(slot, carry):
        rows_ref[pl.ds(slot, 1), :] = cells_ref[pl.ds(chosen_ref[slot], 1), :]
        return carry

    lax.fori_loop(0, parts * each, one, 0, unroll=8)
    for part in range(parts):
        for n in range(planes):
            out_ref[part, n] = rows_ref[part * each : (part + 1) * each, n * plane : (n + 1) * plane]


def gather(chosen, cells, shape):
    return pl.pallas_call(
        gather_kernel,
        in_specs=[pl.BlockSpec(memory_space=pltpu.SMEM), pl.BlockSpec(memory_space=pltpu.VMEM)],
        out_specs=pl.BlockSpec(memory_space=pltpu.VMEM),
        out_shape=jax.ShapeDtypeStruct(shape, jnp.float32),
        scratch_shapes=[pltpu.VMEM((shape[0] * shape[2], cells.shape[1]), jnp.float32)],
    )(chosen, cells)


def scatter_kernel(chosen_ref, count_ref, cells_ref, change_ref, out_ref, rows_ref):
    parts, planes, each, plane = change_ref.shape
    for part in range(parts):
        for n in range(planes):
            rows_ref[part * each : (part + 1) * each, n * plane : (n + 1) * plane] = change_ref[part, n]
    out_ref[...] = cells_ref[...]

    def one(slot, carry):
        row = pl.ds(chosen_ref[slot], 1)
        out_ref[row, :] = cells_ref[row, :] + rows_ref[pl.ds(slot, 1), :]
        return carry

    lax.fori_loop(0, count_ref[0], one, 0)


def scatter(chosen, count, cells, change):
    smem = pl.BlockSpec(memory_space=pltpu.SMEM)
    vmem = pl.BlockSpec(memory_space=pltpu.VMEM)
    return pl.pallas_call(
        scatter_kernel,
        in_specs=[smem, smem, vmem, vmem],
        out_specs=vmem,
        out_shape=jax.ShapeDtypeStruct(cells.shape, jnp.float32),
        scratch_shapes=[pltpu.VMEM((change.shape[0] * change.shape[2], cells.shape[1]), jnp.float32)],
    )(chosen, count, cells, change)


def halves(table):
    high = table.astype(jnp.bfloat16)
    low = (table - high.astype(jnp.float32)).astype(jnp.bfloat16)
    return high, low


def dot3(left, right):
    def dot(a, b):
        return jnp.dot(a, b, preferred_element_type=jnp.float32)

    return dot(left[0], right[0]) + (dot(left[1], right[0]) + dot(left[0], right[1]))


def collide_kernel(cells_ref, first_ref, second_ref, loss_ref, plane_ref, line_ref, out_ref):
    depth, group, plane = cells_ref.shape
    terms = first_ref.shape[0]
    plane_table = (plane_ref[0], plane_ref[1])
    line_table = (line_ref[0], line_ref[1])

    def transform(flat):
        return dot3(line_table, halves(dot3(halves(flat), plane_table)))

    values = cells_ref[...].reshape(depth * group, plane)
    spectrum = transform(values).reshape(depth, group, plane)

    def image(multiplier):
        return transform((spectrum * multiplier[:, None, :]).reshape(depth * group, plane))

    total = -values * image(loss_ref[...])

    def one(term, total):
        return total + image(first_ref[term]) * image(second_ref[term])

    total = lax.fori_loop(0, terms, one, total)
    out_ref[...] = total.reshape(depth, group, plane)


def hartley_tables(vdim):
    index = np.arange(vdim, dtype=np.float64)
    angle = 2.0 * np.pi * np.outer(index, index) / vdim
    table = (np.cos(angle) + np.sin(angle)) / np.sqrt(vdim)

    def split(wide):
        wide = wide.astype(np.float32)
        high = wide.astype(jnp.bfloat16)
        return np.stack([high, (wide - high.astype(np.float32)).astype(jnp.bfloat16)])

    return split(np.kron(table, table)), split(np.kron(table, np.eye(GROUP)))


def collide(cells, gain_first, gain_second, loss_rates):
    depth, count, plane = cells.shape
    spare = -count % GROUP
    if spare:
        cells = jnp.pad(cells, ((0, 0), (0, spare), (0, 0)))
    terms = gain_first.shape[0]
    plane_table, line_table = hartley_tables(VDIM)
    cell_spec = pl.BlockSpec((depth, GROUP, plane), lambda n: (0, n, 0))

    def whole(shape):
        return pl.BlockSpec(shape, lambda n: (0,) * len(shape))

    multipliers = (
        gain_first.reshape(terms, depth, plane),
        gain_second.reshape(terms, depth, plane),
        loss_rates.reshape(depth, plane),
    )
    tables = (jnp.asarray(plane_table), jnp.asarray(line_table))
    result = pl.pallas_call(
        collide_kernel,
        grid=((count + spare) // GROUP,),
        in_specs=[cell_spec] + [whole(array.shape) for array in multipliers + tables],
        out_specs=cell_spec,
        out_shape=jax.ShapeDtypeStruct(cells.shape, jnp.float32),
        compiler_params=pltpu.CompilerParams(vmem_limit_bytes=56 * 1024 * 1024),
    )(cells, *multipliers, *tables)
    return result[:, :count]


def shards(
    distribution, neighbours, block_level, collide_mask, gain_first, gain_second, loss_rates
):
    blocks, cell_count, width = distribution.shape
    assert blocks == 1
    density = distribution.reshape(cell_count, width)
    speeds = speed_rows(lax.axis_index("vel") * width, width)
    ratio = courant * jnp.exp2(block_level.astype(jnp.float32))
    offset = neighbours[0] - (lax.axis_index("space") - 1)
    source = (offset[:, None] == jnp.arange(3)) & (neighbours[0] >= 0)[:, None]
    source = source.astype(jnp.float32).reshape(-1)

    section_one, strips = stage(False, source, ratio, (density, *exchange(pack(density)), speeds))
    section_two = stage(True, source, ratio, (density, section_one, *exchange(strips), speeds))

    parts = lax.axis_size("vel")
    each = ACT // parts
    cell_index = jnp.arange(cell_count)
    rank = jnp.sum(jnp.where(cell_index[:, None] < cell_index, collide_mask[:, None], 0), axis=0)
    hit = (rank[:, None] == jnp.arange(ACT)) & (collide_mask > 0)[:, None]
    chosen = jnp.sum(jnp.where(hit, cell_index[:, None], 0), axis=0)
    held = jnp.sum(collide_mask)[None]

    plane = VDIM * VDIM
    if width % plane == 0:
        planes, span = width // plane, plane
    else:
        planes, span = 1, width
    sent = gather(chosen, section_two, (parts, planes, each, span))
    got = lax.all_to_all(sent, "vel", split_axis=0, concat_axis=0, tiled=True)
    got = got.reshape(parts * planes, each, span)
    if span != plane:
        got = jnp.transpose(got, (1, 0, 2)).reshape(each, VDIM, plane).transpose(1, 0, 2)
    change = collide(got, gain_first, gain_second, loss_rates)
    if span != plane:
        change = change.transpose(1, 0, 2).reshape(each, parts, span).transpose(1, 0, 2)
    change = change.reshape(parts, planes, each, span)
    change = lax.all_to_all(change, "vel", split_axis=0, concat_axis=0, tiled=True)
    return scatter(chosen, held, section_two, change).reshape(blocks, cell_count, width)


def solution(mesh):
    in_specs = (P("space", None, "vel"), P("space", None), P("space"), P("space"), P(), P(), P())
    out_specs = P("space", None, "vel")
    return jax.shard_map(shards, mesh=mesh, in_specs=in_specs, out_specs=out_specs, check_vma=False)
```

```python
import functools

import jax
import jax.numpy as jnp
import numpy as np
from jax import lax
from jax.experimental import pallas as pl
from jax.experimental.pallas import tpu as pltpu
from jax.sharding import PartitionSpec as P

BSIDE = 16
VDIM = 24
ACT = 128
LANES = 128
GROUP = 8


weno_eps = 1e-06
courant = 0.2


def speed_rows(vel_start, vel_width):
    index = vel_start + jnp.arange(vel_width, dtype=jnp.int32)
    half = (VDIM - 1) / 2.0
    first = ((index // (VDIM * VDIM)).astype(jnp.float32) - half) / half
    second = ((index // VDIM % VDIM).astype(jnp.float32) - half) / half
    rows = [jnp.abs(first), jnp.abs(second), jnp.where(first < 0, 1.0, 0.0), jnp.where(second < 0, 1.0, 0.0)]
    return jnp.stack(rows + [jnp.zeros_like(first)] * 4)


def pack_strips(cells_ref, against_first, against_second, strips_ref):
    side = BSIDE

    def first(n):
        return cells_ref[n * side : (n + 1) * side]

    def second(n):
        return cells_ref[pl.ds(n, side, stride=side), :]

    at = 0
    for line, against in ((first, against_first), (second, against_second)):
        far = jnp.where(against, line(2), line(side - 3))
        for layer in (line(0), line(1), far, line(side - 2), line(side - 1)):
            strips_ref[at : at + side] = layer
            at += side


def sweep(line, against, speed, flux_ref):
    side = BSIDE

    def oriented(n):
        return jnp.where(against, line(side + 5 - n), line(n))

    values = [oriented(n) for n in range(4)]
    slopes = [values[n + 1] - values[n] for n in range(3)]
    bends = []
    for n in range(2):
        bend = slopes[n + 1] - slopes[n]
        bends.append(bend * bend * (13.0 / 3.0) + 4.0 * weno_eps)
    before = None
    for i in range(side + 1):
        values.append(oriented(i + 4))
        slopes.append(values[i + 4] - values[i + 3])
        bend = slopes[i + 3] - slopes[i + 2]
        bends.append(bend * bend * (13.0 / 3.0) + 4.0 * weno_eps)
        d0, d1, d2, d3 = slopes[i : i + 4]
        tilt_low = 3.0 * d1 - d0
        tilt_mid = d1 + d2
        tilt_high = d3 - 3.0 * d2
        rough_low = bends[i] + tilt_low * tilt_low
        rough_mid = bends[i + 1] + tilt_mid * tilt_mid
        rough_high = bends[i + 2] + tilt_high * tilt_high
        low2 = rough_low * rough_low
        mid2 = rough_mid * rough_mid
        high2 = rough_high * rough_high
        weight_low = mid2 * high2
        low3 = 3.0 * low2
        weight_mid = (low3 + low3) * high2
        weight_high = low3 * mid2
        guess_low = 5.0 * d1 - 2.0 * d0
        guess_mid = d1 + (d2 + d2)
        guess_high = 4.0 * d2 - d3
        above = weight_low * guess_low + weight_mid * guess_mid + weight_high * guess_high
        below = weight_low + weight_mid + weight_high
        edge = values[i + 2] + above / (6.0 * below)
        if before is not None:
            flux_ref[(i - 1) * side : i * side] = speed * (edge - before)
        before = edge


def advance(source_ref, ratio, u_ref, base_ref, left_ref, right_ref, speed_ref, out_ref, fluxes):
    side = BSIDE
    lanes = u_ref.shape[1]
    flux_one, flux_two, flux_turned = fluxes

    def first_line(n):
        return u_ref[n * side : (n + 1) * side]

    def second_line(n):
        return u_ref[pl.ds(n, side, stride=side), :]

    def ghost(face, block, own):
        at = block * side
        return (
            source_ref[3 * face] * left_ref[at : at + side]
            + source_ref[3 * face + 1] * own
            + source_ref[3 * face + 2] * right_ref[at : at + side]
        )

    def padded(line, faces, start):
        ghosts = {}
        for layer in range(3):
            ghosts[layer] = ghost(faces[0], start + 2 + layer, line(side - 3 + layer))
            ghosts[side + 3 + layer] = ghost(faces[1], start + layer, line(layer))
        return lambda n: ghosts[n] if n in ghosts else line(n - 3)

    against_first, against_second = against_masks(speed_ref)
    sweep(padded(first_line, (0, 1), 0), against_first, spread(speed_ref, 0), flux_one)
    sweep(padded(second_line, (2, 3), 5), against_second, spread(speed_ref, 1), flux_two)
    for n in range(side):
        back = side - 1 - n
        flux_turned[n * side : (n + 1) * side] = jnp.where(
            against_second, flux_two[back * side : (back + 1) * side], flux_two[n * side : (n + 1) * side]
        )
    for n in range(side):
        back = side - 1 - n
        rows = slice(n * side, (n + 1) * side)
        change = jnp.where(against_first, flux_one[back * side : (back + 1) * side], flux_one[rows])
        change = change + flux_turned[pl.ds(n, side, stride=side), :]
        moved = u_ref[rows] - ratio * change
        if base_ref is not None:
            moved = 0.5 * base_ref[rows] + 0.5 * moved
        out_ref[rows] = moved


def spread(speed_ref, row):
    return jnp.broadcast_to(speed_ref[row : row + 1], (BSIDE, speed_ref.shape[1]))


def against_masks(speed_ref):
    return spread(speed_ref, 2) > 0.5, spread(speed_ref, 3) > 0.5


def transport_kernel(
    source_ref, ratio_ref, u_ref, speed_ref, out_ref,
    one_ref, flux_one, flux_two, flux_turned,
    strips, from_left, from_right, sent_left, sent_right, got_left, got_right,
):
    tiles = u_ref.shape[0]
    me = lax.axis_index("space")
    count = lax.axis_size("space")
    has_left, has_right = me > 0, me < count - 1
    left, right = lax.rem(me + count - 1, count), lax.rem(me + 1, count)
    mesh_ids = pl.DeviceIdType.MESH
    ratio = ratio_ref[0]
    fluxes = (flux_one, flux_two, flux_turned)

    barrier = pltpu.get_barrier_semaphore()

    @pl.when(has_left)
    def _():
        pl.semaphore_signal(barrier, inc=1, device_id={"space": left}, device_id_type=mesh_ids)

    @pl.when(has_right)
    def _():
        pl.semaphore_signal(barrier, inc=1, device_id={"space": right}, device_id_type=mesh_ids)

    pl.semaphore_wait(barrier, has_left.astype(jnp.int32) + has_right.astype(jnp.int32))

    def to_right(turn, tile):
        return pltpu.make_async_remote_copy(
            src_ref=strips.at[turn, tile], dst_ref=from_left.at[turn, tile],
            send_sem=sent_right.at[turn, tile], recv_sem=got_left.at[turn, tile],
            device_id={"space": right}, device_id_type=mesh_ids,
        )

    def to_left(turn, tile):
        return pltpu.make_async_remote_copy(
            src_ref=strips.at[turn, tile], dst_ref=from_right.at[turn, tile],
            send_sem=sent_left.at[turn, tile], recv_sem=got_right.at[turn, tile],
            device_id={"space": left}, device_id_type=mesh_ids,
        )

    def send(turn, tile, cells_ref):
        pack_strips(cells_ref.at[tile], *against_masks(speed_ref.at[tile]), strips.at[turn, tile])

        @pl.when(has_right)
        def _():
            to_right(turn, tile).start()

        @pl.when(has_left)
        def _():
            to_left(turn, tile).start()

    def receive(turn, tile):
        @pl.when(has_left)
        def _():
            to_right(turn, tile).wait_recv()

        @pl.when(has_right)
        def _():
            to_left(turn, tile).wait_recv()

    def begin(tile, carry):
        send(0, tile, u_ref)
        return carry

    lax.fori_loop(0, tiles, begin, 0)

    @pl.when(me == 0)
    def _():
        from_left[...] = jnp.zeros_like(from_left)

    @pl.when(me == count - 1)
    def _():
        from_right[...] = jnp.zeros_like(from_right)

    def first(tile, carry):
        receive(0, tile)
        advance(
            source_ref, ratio, u_ref.at[tile], None, from_left.at[0, tile], from_right.at[0, tile],
            speed_ref.at[tile], one_ref.at[tile], fluxes,
        )
        send(1, tile, one_ref)
        return carry

    lax.fori_loop(0, tiles, first, 0)

    def second(tile, carry):
        receive(1, tile)
        advance(
            source_ref, ratio, one_ref.at[tile], u_ref.at[tile], from_left.at[1, tile], from_right.at[1, tile],
            speed_ref.at[tile], out_ref.at[tile], fluxes,
        )
        return carry

    lax.fori_loop(0, tiles, second, 0)

    def finish(tile, carry):
        for turn in range(2):

            @pl.when(has_right)
            def _():
                to_right(turn, tile).wait_send()

            @pl.when(has_left)
            def _():
                to_left(turn, tile).wait_send()

        return carry

    lax.fori_loop(0, tiles, finish, 0)


def transport(source, ratio, cells, speeds):
    tiles, count, lanes = cells.shape
    smem = pl.BlockSpec(memory_space=pltpu.SMEM)
    vmem = pl.BlockSpec(memory_space=pltpu.VMEM)
    strips = pltpu.VMEM((2, tiles, 10 * BSIDE, lanes), jnp.float32)
    return pl.pallas_call(
        transport_kernel,
        in_specs=[smem, smem, vmem, vmem],
        out_specs=vmem,
        out_shape=jax.ShapeDtypeStruct(cells.shape, jnp.float32),
        scratch_shapes=[pltpu.VMEM(cells.shape, jnp.float32)]
        + [pltpu.VMEM((count, lanes), jnp.float32)] * 3
        + [strips] * 3
        + [pltpu.SemaphoreType.DMA((2, tiles))] * 4,
        compiler_params=pltpu.CompilerParams(
            collective_id=0, has_side_effects=True, vmem_limit_bytes=48 * 1024 * 1024
        ),
    )(source, ratio, cells, speeds)


def tiled(rows):
    count, width = rows.shape
    tiles = pl.cdiv(width, LANES)
    rows = jnp.pad(rows, ((0, 0), (0, tiles * LANES - width)))
    return rows.reshape(count, tiles, LANES).transpose(1, 0, 2)


def lane_pieces(tiles, width):
    return [(t, t * LANES, min(width, (t + 1) * LANES)) for t in range(tiles)]


def gather_kernel(chosen_ref, cells_ref, out_ref, picked_ref, rows_ref):
    parts, planes, each, plane = out_ref.shape
    tiles = cells_ref.shape[0]

    def one(slot, carry):
        row = chosen_ref[slot]
        for tile in range(tiles):
            picked_ref[tile, pl.ds(slot, 1), :] = cells_ref[tile, pl.ds(row, 1), :]
        return carry

    lax.fori_loop(0, parts * each, one, 0, unroll=8)
    for tile in range(tiles):
        rows_ref[:, tile * LANES : (tile + 1) * LANES] = picked_ref[tile]
    for part in range(parts):
        for n in range(planes):
            out_ref[part, n] = rows_ref[part * each : (part + 1) * each, n * plane : (n + 1) * plane]


def gather(chosen, cells, shape):
    return pl.pallas_call(
        gather_kernel,
        in_specs=[pl.BlockSpec(memory_space=pltpu.SMEM), pl.BlockSpec(memory_space=pltpu.VMEM)],
        out_specs=pl.BlockSpec(memory_space=pltpu.VMEM),
        out_shape=jax.ShapeDtypeStruct(shape, jnp.float32),
        scratch_shapes=[
            pltpu.VMEM((cells.shape[0], shape[0] * shape[2], LANES), jnp.float32),
            pltpu.VMEM((shape[0] * shape[2], cells.shape[0] * LANES), jnp.float32),
        ],
    )(chosen, cells)


def scatter_kernel(chosen_ref, count_ref, cells_ref, change_ref, out_ref, rows_ref):
    parts, planes, each, plane = change_ref.shape
    for tile, begin, end in lane_pieces(cells_ref.shape[0], out_ref.shape[1]):
        out_ref[:, begin:end] = cells_ref[tile, :, : end - begin]
    for part in range(parts):
        for n in range(planes):
            rows_ref[part * each : (part + 1) * each, n * plane : (n + 1) * plane] = change_ref[part, n]

    def one(slot, carry):
        row = pl.ds(chosen_ref[slot], 1)
        out_ref[row, :] += rows_ref[pl.ds(slot, 1), :]
        return carry

    lax.fori_loop(0, count_ref[0], one, 0)


def scatter(chosen, count, cells, change):
    smem = pl.BlockSpec(memory_space=pltpu.SMEM)
    vmem = pl.BlockSpec(memory_space=pltpu.VMEM)
    parts, planes, each, plane = change.shape
    return pl.pallas_call(
        scatter_kernel,
        in_specs=[smem, smem, vmem, vmem],
        out_specs=vmem,
        out_shape=jax.ShapeDtypeStruct((cells.shape[1], planes * plane), jnp.float32),
        scratch_shapes=[pltpu.VMEM((parts * each, planes * plane), jnp.float32)],
    )(chosen, count, cells, change)


def halves(table):
    high = table.astype(jnp.bfloat16)
    low = (table - high.astype(jnp.float32)).astype(jnp.bfloat16)
    return high, low


def dot(left, right):
    return jnp.dot(left, right, preferred_element_type=jnp.float32)


def collide_kernel(cells_ref, first_ref, second_ref, loss_ref, plane_ref, line_ref, out_ref):
    depth, group, plane = cells_ref.shape
    terms = first_ref.shape[0]
    size = depth * group

    def transforms(cubes):
        high, low = halves(jnp.concatenate(cubes, axis=0) if len(cubes) > 1 else cubes[0])
        rows = high.shape[0]
        wide = dot(jnp.concatenate([high, low], axis=0), plane_ref[0])
        mapped = wide[:rows] + (wide[rows:] + dot(high, plane_ref[1]))
        results = []
        for n in range(len(cubes)):
            high, low = halves(mapped[n * size : (n + 1) * size])
            wide = dot(line_ref[...], high)
            results.append(wide[:size] + (wide[size:] + dot(line_ref[:size], low)))
        return results

    values = cells_ref[...].reshape(size, plane)
    spectrum = transforms([values])[0].reshape(depth, group, plane)

    def scaled(multiplier):
        return (spectrum * multiplier[:, None, :]).reshape(size, plane)

    total = -values * transforms([scaled(loss_ref[...])])[0]

    def one(term, total):
        image_one, image_two = transforms([scaled(first_ref[term]), scaled(second_ref[term])])
        return total + image_one * image_two

    total = lax.fori_loop(0, terms, one, total)
    out_ref[...] = total.reshape(depth, group, plane)


def hartley_tables(vdim):
    index = np.arange(vdim, dtype=np.float64)
    angle = 2.0 * np.pi * np.outer(index, index) / vdim
    table = (np.cos(angle) + np.sin(angle)) / np.sqrt(vdim)

    def split(wide):
        wide = wide.astype(np.float32)
        high = wide.astype(jnp.bfloat16)
        return np.stack([high, (wide - high.astype(np.float32)).astype(jnp.bfloat16)])

    return split(np.kron(table, table)), np.concatenate(split(np.kron(table, np.eye(GROUP))))


def collide(cells, gain_first, gain_second, loss_rates):
    depth, count, plane = cells.shape
    spare = -count % GROUP
    if spare:
        cells = jnp.pad(cells, ((0, 0), (0, spare), (0, 0)))
    terms = gain_first.shape[0]
    plane_table, line_table = hartley_tables(VDIM)
    cell_spec = pl.BlockSpec((depth, GROUP, plane), lambda n: (0, n, 0))

    def whole(shape):
        return pl.BlockSpec(shape, lambda n: (0,) * len(shape))

    multipliers = (
        gain_first.reshape(terms, depth, plane),
        gain_second.reshape(terms, depth, plane),
        loss_rates.reshape(depth, plane),
    )
    tables = (jnp.asarray(plane_table), jnp.asarray(line_table))
    result = pl.pallas_call(
        collide_kernel,
        grid=((count + spare) // GROUP,),
        in_specs=[cell_spec] + [whole(array.shape) for array in multipliers + tables],
        out_specs=cell_spec,
        out_shape=jax.ShapeDtypeStruct(cells.shape, jnp.float32),
        compiler_params=pltpu.CompilerParams(vmem_limit_bytes=56 * 1024 * 1024),
    )(cells, *multipliers, *tables)
    return result[:, :count]


def shards(
    distribution, neighbours, block_level, collide_mask, gain_first, gain_second, loss_rates
):
    blocks, cell_count, width = distribution.shape
    assert blocks == 1
    density = distribution.reshape(cell_count, width)
    speeds = speed_rows(lax.axis_index("vel") * width, width)
    ratio = courant * jnp.exp2(block_level.astype(jnp.float32))
    offset = neighbours[0] - (lax.axis_index("space") - 1)
    source = (offset[:, None] == jnp.arange(3)) & (neighbours[0] >= 0)[:, None]
    source = source.astype(jnp.float32).reshape(-1)

    section_two = transport(source, ratio, tiled(density), tiled(speeds))

    parts = lax.axis_size("vel")
    each = ACT // parts
    cell_index = jnp.arange(cell_count)
    rank = jnp.sum(jnp.where(cell_index[:, None] < cell_index, collide_mask[:, None], 0), axis=0)
    hit = (rank[:, None] == jnp.arange(ACT)) & (collide_mask > 0)[:, None]
    chosen = jnp.sum(jnp.where(hit, cell_index[:, None], 0), axis=0)
    held = jnp.sum(collide_mask)[None]

    plane = VDIM * VDIM
    if width % plane == 0:
        planes, span = width // plane, plane
    else:
        planes, span = 1, width
    sent = gather(chosen, section_two, (parts, planes, each, span))
    got = lax.all_to_all(sent, "vel", split_axis=0, concat_axis=0, tiled=True)
    got = got.reshape(parts * planes, each, span)
    if span != plane:
        got = jnp.transpose(got, (1, 0, 2)).reshape(each, VDIM, plane).transpose(1, 0, 2)
    change = collide(got, gain_first, gain_second, loss_rates)
    if span != plane:
        change = change.transpose(1, 0, 2).reshape(each, parts, span).transpose(1, 0, 2)
    change = change.reshape(parts, planes, each, span)
    change = lax.all_to_all(change, "vel", split_axis=0, concat_axis=0, tiled=True)
    return scatter(chosen, held, section_two, change).reshape(blocks, cell_count, width)


def solution(mesh):
    in_specs = (P("space", None, "vel"), P("space", None), P("space"), P("space"), P(), P(), P())
    out_specs = P("space", None, "vel")
    return jax.shard_map(shards, mesh=mesh, in_specs=in_specs, out_specs=out_specs, check_vma=False)
```

```python
import functools

import jax
import jax.numpy as jnp
import numpy as np
from jax import lax
from jax.experimental import pallas as pl
from jax.experimental.pallas import tpu as pltpu
from jax.sharding import PartitionSpec as P

BSIDE = 16
VDIM = 24
ACT = 128
LANES = 128
GROUP = 8


weno_eps = 1e-06
courant = 0.2


def speed_rows(vel_start, vel_width):
    index = vel_start + jnp.arange(vel_width, dtype=jnp.int32)
    half = (VDIM - 1) / 2.0
    first = ((index // (VDIM * VDIM)).astype(jnp.float32) - half) / half
    second = ((index // VDIM % VDIM).astype(jnp.float32) - half) / half
    rows = [jnp.abs(first), jnp.abs(second), jnp.where(first < 0, 1.0, 0.0), jnp.where(second < 0, 1.0, 0.0)]
    return jnp.stack(rows + [jnp.zeros_like(first)] * 4)


def pack_strips(cells_ref, against_first, against_second, strips_ref):
    side = BSIDE

    def first(n):
        return cells_ref[n * side : (n + 1) * side]

    def second(n):
        return cells_ref[pl.ds(n, side, stride=side), :]

    at = 0
    for line, against in ((first, against_first), (second, against_second)):
        far = jnp.where(against, line(2), line(side - 3))
        for layer in (line(0), line(1), far, line(side - 2), line(side - 1)):
            strips_ref[at : at + side] = layer
            at += side


def sweep(line, against, speed, flux_ref):
    side = BSIDE

    def oriented(n):
        return jnp.where(against, line(side + 5 - n), line(n))

    values = [oriented(n) for n in range(4)]
    slopes = [values[n + 1] - values[n] for n in range(3)]
    bends = []
    for n in range(2):
        bend = slopes[n + 1] - slopes[n]
        bends.append(bend * bend * (13.0 / 3.0) + 4.0 * weno_eps)
    before = None
    for i in range(side + 1):
        values.append(oriented(i + 4))
        slopes.append(values[i + 4] - values[i + 3])
        bend = slopes[i + 3] - slopes[i + 2]
        bends.append(bend * bend * (13.0 / 3.0) + 4.0 * weno_eps)
        d0, d1, d2, d3 = slopes[i : i + 4]
        tilt_low = 3.0 * d1 - d0
        tilt_mid = d1 + d2
        tilt_high = d3 - 3.0 * d2
        rough_low = bends[i] + tilt_low * tilt_low
        rough_mid = bends[i + 1] + tilt_mid * tilt_mid
        rough_high = bends[i + 2] + tilt_high * tilt_high
        low2 = rough_low * rough_low
        mid2 = rough_mid * rough_mid
        high2 = rough_high * rough_high
        weight_low = mid2 * high2
        low3 = 3.0 * low2
        weight_mid = (low3 + low3) * high2
        weight_high = low3 * mid2
        guess_low = 5.0 * d1 - 2.0 * d0
        guess_mid = d1 + (d2 + d2)
        guess_high = 4.0 * d2 - d3
        above = weight_low * guess_low + weight_mid * guess_mid + weight_high * guess_high
        below = weight_low + weight_mid + weight_high
        edge = values[i + 2] + above / (6.0 * below)
        if before is not None:
            flux_ref[(i - 1) * side : i * side] = speed * (edge - before)
        before = edge


def advance(source_ref, ratio, u_ref, base_ref, left_ref, right_ref, speed_ref, out_ref, fluxes):
    side = BSIDE
    lanes = u_ref.shape[1]
    flux_one, flux_two, flux_turned = fluxes

    def first_line(n):
        return u_ref[n * side : (n + 1) * side]

    def second_line(n):
        return u_ref[pl.ds(n, side, stride=side), :]

    def ghost(face, block, own):
        at = block * side
        return (
            source_ref[3 * face] * left_ref[at : at + side]
            + source_ref[3 * face + 1] * own
            + source_ref[3 * face + 2] * right_ref[at : at + side]
        )

    def padded(line, faces, start):
        ghosts = {}
        for layer in range(3):
            ghosts[layer] = ghost(faces[0], start + 2 + layer, line(side - 3 + layer))
            ghosts[side + 3 + layer] = ghost(faces[1], start + layer, line(layer))
        return lambda n: ghosts[n] if n in ghosts else line(n - 3)

    against_first, against_second = against_masks(speed_ref)
    sweep(padded(first_line, (0, 1), 0), against_first, spread(speed_ref, 0), flux_one)
    sweep(padded(second_line, (2, 3), 5), against_second, spread(speed_ref, 1), flux_two)
    for n in range(side):
        back = side - 1 - n
        flux_turned[n * side : (n + 1) * side] = jnp.where(
            against_second, flux_two[back * side : (back + 1) * side], flux_two[n * side : (n + 1) * side]
        )
    for n in range(side):
        back = side - 1 - n
        rows = slice(n * side, (n + 1) * side)
        change = jnp.where(against_first, flux_one[back * side : (back + 1) * side], flux_one[rows])
        change = change + flux_turned[pl.ds(n, side, stride=side), :]
        moved = u_ref[rows] - ratio * change
        if base_ref is not None:
            moved = 0.5 * base_ref[rows] + 0.5 * moved
        out_ref[rows] = moved


def spread(speed_ref, row):
    return jnp.broadcast_to(speed_ref[row : row + 1], (BSIDE, speed_ref.shape[1]))


def against_masks(speed_ref):
    return spread(speed_ref, 2) > 0.5, spread(speed_ref, 3) > 0.5


def transport_kernel(
    source_ref, ratio_ref, u_ref, speed_ref, out_ref,
    one_ref, flux_one, flux_two, flux_turned,
    strips, from_left, from_right, sent_left, sent_right, got_left, got_right,
):
    tiles = u_ref.shape[0]
    me = lax.axis_index("space")
    count = lax.axis_size("space")
    has_left, has_right = me > 0, me < count - 1
    left, right = lax.rem(me + count - 1, count), lax.rem(me + 1, count)
    mesh_ids = pl.DeviceIdType.MESH
    ratio = ratio_ref[0]
    fluxes = (flux_one, flux_two, flux_turned)

    barrier = pltpu.get_barrier_semaphore()

    @pl.when(has_left)
    def _():
        pl.semaphore_signal(barrier, inc=1, device_id={"space": left}, device_id_type=mesh_ids)

    @pl.when(has_right)
    def _():
        pl.semaphore_signal(barrier, inc=1, device_id={"space": right}, device_id_type=mesh_ids)

    pl.semaphore_wait(barrier, has_left.astype(jnp.int32) + has_right.astype(jnp.int32))

    def to_right(turn, tile):
        return pltpu.make_async_remote_copy(
            src_ref=strips.at[turn, tile], dst_ref=from_left.at[turn, tile],
            send_sem=sent_right.at[turn, tile], recv_sem=got_left.at[turn, tile],
            device_id={"space": right}, device_id_type=mesh_ids,
        )

    def to_left(turn, tile):
        return pltpu.make_async_remote_copy(
            src_ref=strips.at[turn, tile], dst_ref=from_right.at[turn, tile],
            send_sem=sent_left.at[turn, tile], recv_sem=got_right.at[turn, tile],
            device_id={"space": left}, device_id_type=mesh_ids,
        )

    def send(turn, tile, cells_ref):
        pack_strips(cells_ref.at[tile], *against_masks(speed_ref.at[tile]), strips.at[turn, tile])

        @pl.when(has_right)
        def _():
            to_right(turn, tile).start()

        @pl.when(has_left)
        def _():
            to_left(turn, tile).start()

    def receive(turn, tile):
        @pl.when(has_left)
        def _():
            to_right(turn, tile).wait_recv()

        @pl.when(has_right)
        def _():
            to_left(turn, tile).wait_recv()

    def begin(tile, carry):
        send(0, tile, u_ref)
        return carry

    lax.fori_loop(0, tiles, begin, 0)

    @pl.when(me == 0)
    def _():
        from_left[...] = jnp.zeros_like(from_left)

    @pl.when(me == count - 1)
    def _():
        from_right[...] = jnp.zeros_like(from_right)

    def first(tile, carry):
        receive(0, tile)
        advance(
            source_ref, ratio, u_ref.at[tile], None, from_left.at[0, tile], from_right.at[0, tile],
            speed_ref.at[tile], one_ref.at[tile], fluxes,
        )
        send(1, tile, one_ref)
        return carry

    lax.fori_loop(0, tiles, first, 0)

    def second(tile, carry):
        receive(1, tile)
        advance(
            source_ref, ratio, one_ref.at[tile], u_ref.at[tile], from_left.at[1, tile], from_right.at[1, tile],
            speed_ref.at[tile], out_ref.at[tile], fluxes,
        )
        return carry

    lax.fori_loop(0, tiles, second, 0)

    def finish(tile, carry):
        for turn in range(2):

            @pl.when(has_right)
            def _():
                to_right(turn, tile).wait_send()

            @pl.when(has_left)
            def _():
                to_left(turn, tile).wait_send()

        return carry

    lax.fori_loop(0, tiles, finish, 0)


def transport(source, ratio, cells, speeds):
    tiles, count, lanes = cells.shape
    smem = pl.BlockSpec(memory_space=pltpu.SMEM)
    vmem = pl.BlockSpec(memory_space=pltpu.VMEM)
    strips = pltpu.VMEM((2, tiles, 10 * BSIDE, lanes), jnp.float32)
    return pl.pallas_call(
        transport_kernel,
        in_specs=[smem, smem, vmem, vmem],
        out_specs=vmem,
        out_shape=jax.ShapeDtypeStruct(cells.shape, jnp.float32),
        scratch_shapes=[pltpu.VMEM(cells.shape, jnp.float32)]
        + [pltpu.VMEM((count, lanes), jnp.float32)] * 3
        + [strips] * 3
        + [pltpu.SemaphoreType.DMA((2, tiles))] * 4,
        compiler_params=pltpu.CompilerParams(
            collective_id=0, has_side_effects=True, vmem_limit_bytes=48 * 1024 * 1024
        ),
    )(source, ratio, cells, speeds)


def tiled(rows):
    count, width = rows.shape
    tiles = pl.cdiv(width, LANES)
    rows = jnp.pad(rows, ((0, 0), (0, tiles * LANES - width)))
    return rows.reshape(count, tiles, LANES).transpose(1, 0, 2)


def lane_pieces(tiles, width):
    return [(t, t * LANES, min(width, (t + 1) * LANES)) for t in range(tiles)]


def gather_kernel(chosen_ref, cells_ref, out_ref, picked_ref, rows_ref):
    parts, planes, each, plane = out_ref.shape
    tiles = cells_ref.shape[0]

    def one(slot, carry):
        row = chosen_ref[slot]
        for tile in range(tiles):
            picked_ref[tile, pl.ds(slot, 1), :] = cells_ref[tile, pl.ds(row, 1), :]
        return carry

    lax.fori_loop(0, parts * each, one, 0, unroll=8)
    for tile in range(tiles):
        rows_ref[:, tile * LANES : (tile + 1) * LANES] = picked_ref[tile]
    for part in range(parts):
        for n in range(planes):
            out_ref[part, n] = rows_ref[part * each : (part + 1) * each, n * plane : (n + 1) * plane]


def gather(chosen, cells, shape):
    return pl.pallas_call(
        gather_kernel,
        in_specs=[pl.BlockSpec(memory_space=pltpu.SMEM), pl.BlockSpec(memory_space=pltpu.VMEM)],
        out_specs=pl.BlockSpec(memory_space=pltpu.VMEM),
        out_shape=jax.ShapeDtypeStruct(shape, jnp.float32),
        scratch_shapes=[
            pltpu.VMEM((cells.shape[0], shape[0] * shape[2], LANES), jnp.float32),
            pltpu.VMEM((shape[0] * shape[2], cells.shape[0] * LANES), jnp.float32),
        ],
    )(chosen, cells)


def scatter_kernel(chosen_ref, count_ref, cells_ref, change_ref, out_ref, rows_ref):
    parts, planes, each, plane = change_ref.shape
    for tile, begin, end in lane_pieces(cells_ref.shape[0], out_ref.shape[1]):
        out_ref[:, begin:end] = cells_ref[tile, :, : end - begin]
    for part in range(parts):
        for n in range(planes):
            rows_ref[part * each : (part + 1) * each, n * plane : (n + 1) * plane] = change_ref[part, n]

    def one(slot, carry):
        row = pl.ds(chosen_ref[slot], 1)
        out_ref[row, :] += rows_ref[pl.ds(slot, 1), :]
        return carry

    lax.fori_loop(0, count_ref[0], one, 0)


def scatter(chosen, count, cells, change):
    smem = pl.BlockSpec(memory_space=pltpu.SMEM)
    vmem = pl.BlockSpec(memory_space=pltpu.VMEM)
    parts, planes, each, plane = change.shape
    return pl.pallas_call(
        scatter_kernel,
        in_specs=[smem, smem, vmem, vmem],
        out_specs=vmem,
        out_shape=jax.ShapeDtypeStruct((cells.shape[1], planes * plane), jnp.float32),
        scratch_shapes=[pltpu.VMEM((parts * each, planes * plane), jnp.float32)],
    )(chosen, count, cells, change)


def halves(table):
    high = table.astype(jnp.bfloat16)
    low = (table - high.astype(jnp.float32)).astype(jnp.bfloat16)
    return high, low


def dot(left, right):
    return jnp.dot(left, right, preferred_element_type=jnp.float32)


def collision(values, tables, depth):
    first_ref, second_ref, loss_ref, plane_ref, line_ref = tables
    size, plane = values.shape
    group = size // depth

    def transforms(cubes):
        high, low = halves(jnp.concatenate(cubes, axis=0) if len(cubes) > 1 else cubes[0])
        rows = high.shape[0]
        wide = dot(jnp.concatenate([high, low], axis=0), plane_ref[0])
        mapped = wide[:rows] + (wide[rows:] + dot(high, plane_ref[1]))
        results = []
        for n in range(len(cubes)):
            high, low = halves(mapped[n * size : (n + 1) * size])
            wide = dot(line_ref[...], high)
            results.append(wide[:size] + (wide[size:] + dot(line_ref[:size], low)))
        return results

    spectrum = transforms([values])[0].reshape(depth, group, plane)

    def scaled(multiplier):
        return (spectrum * multiplier[:, None, :]).reshape(size, plane)

    total = -values * transforms([scaled(loss_ref[...])])[0]

    def one(term, total):
        image_one, image_two = transforms([scaled(first_ref[term]), scaled(second_ref[term])])
        return total + image_one * image_two

    return lax.fori_loop(0, first_ref.shape[0], one, total)


def collide_kernel(cells_ref, *refs):
    depth, group, plane = cells_ref.shape
    out_ref = refs[-1]
    total = collision(cells_ref[...].reshape(depth * group, plane), refs[:-1], depth)
    out_ref[...] = total.reshape(depth, group, plane)


def swap_collide_kernel(
    cells_ref, first_ref, second_ref, loss_ref, plane_ref, line_ref, out_ref,
    got, result, sent_in, got_in, own_in, sent_out, got_out, own_out,
):
    parts = lax.axis_size("vel")
    blocks, planes, group, plane = cells_ref.shape
    chunks = blocks // parts
    me = lax.axis_index("vel")
    mesh_ids = pl.DeviceIdType.MESH
    peers = [lax.rem(me + n, parts) for n in range(parts)]
    tables = (first_ref, second_ref, loss_ref, plane_ref, line_ref)

    barrier = pltpu.get_barrier_semaphore()
    for peer in peers[1:]:
        pl.semaphore_signal(barrier, inc=1, device_id={"vel": peer}, device_id_type=mesh_ids)
    pl.semaphore_wait(barrier, parts - 1)

    def swap(chunk, from_ref, to_ref, send_sem, recv_sem, own_sem):
        mine = chunk * parts + me
        copies = []
        for n, peer in enumerate(peers):
            source = from_ref.at[chunk * parts + peer]
            if n == 0:
                copies.append(pltpu.make_async_copy(source, to_ref.at[mine], own_sem.at[chunk]))
            else:
                copies.append(
                    pltpu.make_async_remote_copy(
                        src_ref=source, dst_ref=to_ref.at[mine],
                        send_sem=send_sem.at[chunk, n], recv_sem=recv_sem.at[chunk, n],
                        device_id={"vel": peer}, device_id_type=mesh_ids,
                    )
                )
            copies[-1].start()
        return copies

    incoming = [swap(chunk, cells_ref, got, sent_in, got_in, own_in) for chunk in range(chunks)]
    outgoing = []
    for chunk in range(chunks):
        for copy in incoming[chunk][1:]:
            copy.wait_recv()
        incoming[chunk][0].wait()
        held = slice(chunk * parts, (chunk + 1) * parts)
        values = got[held].reshape(parts * planes * group, plane)
        result[held] = collision(values, tables, parts * planes).reshape(parts, planes, group, plane)
        outgoing.append(swap(chunk, result, out_ref, sent_out, got_out, own_out))
    for copies in outgoing:
        copies[0].wait()
        for copy in copies[1:]:
            copy.wait_recv()
    for copies in incoming + outgoing:
        for copy in copies[1:]:
            copy.wait_send()


def hartley_tables(vdim):
    index = np.arange(vdim, dtype=np.float64)
    angle = 2.0 * np.pi * np.outer(index, index) / vdim
    table = (np.cos(angle) + np.sin(angle)) / np.sqrt(vdim)

    def split(wide):
        wide = wide.astype(np.float32)
        high = wide.astype(jnp.bfloat16)
        return np.stack([high, (wide - high.astype(np.float32)).astype(jnp.bfloat16)])

    return split(np.kron(table, table)), np.concatenate(split(np.kron(table, np.eye(GROUP))))


def collision_operands(gain_first, gain_second, loss_rates):
    terms, plane = gain_first.shape[0], VDIM * VDIM
    plane_table, line_table = hartley_tables(VDIM)
    return (
        gain_first.reshape(terms, VDIM, plane),
        gain_second.reshape(terms, VDIM, plane),
        loss_rates.reshape(VDIM, plane),
        jnp.asarray(plane_table),
        jnp.asarray(line_table),
    )


def collide(cells, operands):
    depth, count, plane = cells.shape
    spare = -count % GROUP
    if spare:
        cells = jnp.pad(cells, ((0, 0), (0, spare), (0, 0)))
    cell_spec = pl.BlockSpec((depth, GROUP, plane), lambda n: (0, n, 0))

    def whole(shape):
        return pl.BlockSpec(shape, lambda n: (0,) * len(shape))

    result = pl.pallas_call(
        collide_kernel,
        grid=((count + spare) // GROUP,),
        in_specs=[cell_spec] + [whole(array.shape) for array in operands],
        out_specs=cell_spec,
        out_shape=jax.ShapeDtypeStruct(cells.shape, jnp.float32),
        compiler_params=pltpu.CompilerParams(vmem_limit_bytes=56 * 1024 * 1024),
    )(cells, *operands)
    return result[:, :count]


def swap_collide(cells, operands):
    chunks, parts = cells.shape[0] // lax.axis_size("vel"), lax.axis_size("vel")
    vmem = pl.BlockSpec(memory_space=pltpu.VMEM)
    across = pltpu.SemaphoreType.DMA((chunks, parts))
    own = pltpu.SemaphoreType.DMA((chunks,))
    return pl.pallas_call(
        swap_collide_kernel,
        in_specs=[vmem] * (1 + len(operands)),
        out_specs=vmem,
        out_shape=jax.ShapeDtypeStruct(cells.shape, jnp.float32),
        scratch_shapes=[pltpu.VMEM(cells.shape, jnp.float32)] * 2 + [across, across, own] * 2,
        compiler_params=pltpu.CompilerParams(
            collective_id=1, has_side_effects=True, vmem_limit_bytes=56 * 1024 * 1024
        ),
    )(cells, *operands)


def shards(
    distribution, neighbours, block_level, collide_mask, gain_first, gain_second, loss_rates
):
    blocks, cell_count, width = distribution.shape
    assert blocks == 1
    density = distribution.reshape(cell_count, width)
    speeds = speed_rows(lax.axis_index("vel") * width, width)
    ratio = courant * jnp.exp2(block_level.astype(jnp.float32))
    offset = neighbours[0] - (lax.axis_index("space") - 1)
    source = (offset[:, None] == jnp.arange(3)) & (neighbours[0] >= 0)[:, None]
    source = source.astype(jnp.float32).reshape(-1)

    section_two = transport(source, ratio, tiled(density), tiled(speeds))

    parts = lax.axis_size("vel")
    each = ACT // parts
    cell_index = jnp.arange(cell_count)
    rank = jnp.sum(jnp.where(cell_index[:, None] < cell_index, collide_mask[:, None], 0), axis=0)
    hit = (rank[:, None] == jnp.arange(ACT)) & (collide_mask > 0)[:, None]
    chosen = jnp.sum(jnp.where(hit, cell_index[:, None], 0), axis=0)
    held = jnp.sum(collide_mask)[None]

    plane = VDIM * VDIM
    operands = collision_operands(gain_first, gain_second, loss_rates)
    if width % plane == 0 and each % GROUP == 0:
        sent = gather(chosen, section_two, (ACT // GROUP, width // plane, GROUP, plane))
        change = swap_collide(sent, operands)
    else:
        sent = gather(chosen, section_two, (parts, 1, each, width))
        got = lax.all_to_all(sent, "vel", split_axis=0, concat_axis=0, tiled=True)
        got = jnp.transpose(got.reshape(parts, each, width), (1, 0, 2))
        got = got.reshape(each, VDIM, plane).transpose(1, 0, 2)
        change = collide(got, operands).transpose(1, 0, 2).reshape(each, parts, width)
        change = change.transpose(1, 0, 2)[:, None]
        change = lax.all_to_all(change, "vel", split_axis=0, concat_axis=0, tiled=True)
    return scatter(chosen, held, section_two, change).reshape(blocks, cell_count, width)


def solution(mesh):
    in_specs = (P("space", None, "vel"), P("space", None), P("space"), P("space"), P(), P(), P())
    out_specs = P("space", None, "vel")
    return jax.shard_map(shards, mesh=mesh, in_specs=in_specs, out_specs=out_specs, check_vma=False)
```

```python
import functools

import jax
import jax.numpy as jnp
import numpy as np
from jax import lax
from jax.experimental import pallas as pl
from jax.experimental.pallas import tpu as pltpu
from jax.sharding import PartitionSpec as P

BSIDE = 16
VDIM = 24
ACT = 128
LANES = 128
GROUP = 8


weno_eps = 1e-06
courant = 0.2


def speed_rows(vel_start, vel_width):
    index = vel_start + jnp.arange(vel_width, dtype=jnp.int32)
    half = (VDIM - 1) / 2.0
    first = ((index // (VDIM * VDIM)).astype(jnp.float32) - half) / half
    second = ((index // VDIM % VDIM).astype(jnp.float32) - half) / half
    rows = [jnp.abs(first), jnp.abs(second), jnp.where(first < 0, 1.0, 0.0), jnp.where(second < 0, 1.0, 0.0)]
    return jnp.stack(rows + [jnp.zeros_like(first)] * 4)


def pack_strips(cells_ref, against_first, against_second, strips_ref):
    side = BSIDE

    def first(n):
        return cells_ref[n * side : (n + 1) * side]

    def second(n):
        return cells_ref[pl.ds(n, side, stride=side), :]

    at = 0
    for line, against in ((first, against_first), (second, against_second)):
        far = jnp.where(against, line(2), line(side - 3))
        for layer in (line(0), line(1), far, line(side - 2), line(side - 1)):
            strips_ref[at : at + side] = layer
            at += side


def sweep(line, against, speed, flux_ref):
    side = BSIDE

    def oriented(n):
        return jnp.where(against, line(side + 5 - n), line(n))

    values = [oriented(n) for n in range(4)]
    slopes = [values[n + 1] - values[n] for n in range(3)]
    bends = []
    for n in range(2):
        bend = slopes[n + 1] - slopes[n]
        bends.append(bend * bend * (13.0 / 3.0) + 4.0 * weno_eps)
    before = None
    for i in range(side + 1):
        values.append(oriented(i + 4))
        slopes.append(values[i + 4] - values[i + 3])
        bend = slopes[i + 3] - slopes[i + 2]
        bends.append(bend * bend * (13.0 / 3.0) + 4.0 * weno_eps)
        d0, d1, d2, d3 = slopes[i : i + 4]
        tilt_low = 3.0 * d1 - d0
        tilt_mid = d1 + d2
        tilt_high = d3 - 3.0 * d2
        rough_low = bends[i] + tilt_low * tilt_low
        rough_mid = bends[i + 1] + tilt_mid * tilt_mid
        rough_high = bends[i + 2] + tilt_high * tilt_high
        low2 = rough_low * rough_low
        mid2 = rough_mid * rough_mid
        high2 = rough_high * rough_high
        weight_low = mid2 * high2
        low3 = 3.0 * low2
        weight_mid = (low3 + low3) * high2
        weight_high = low3 * mid2
        guess_low = 5.0 * d1 - 2.0 * d0
        guess_mid = d1 + (d2 + d2)
        guess_high = 4.0 * d2 - d3
        above = weight_low * guess_low + weight_mid * guess_mid + weight_high * guess_high
        below = weight_low + weight_mid + weight_high
        edge = values[i + 2] + above / (6.0 * below)
        if before is not None:
            flux_ref[(i - 1) * side : i * side] = speed * (edge - before)
        before = edge


def advance(source_ref, ratio, u_ref, base_ref, left_ref, right_ref, speed_ref, out_ref, fluxes):
    side = BSIDE
    lanes = u_ref.shape[1]
    flux_one, flux_two, flux_turned = fluxes

    def first_line(n):
        return u_ref[n * side : (n + 1) * side]

    def second_line(n):
        return u_ref[pl.ds(n, side, stride=side), :]

    def ghost(face, block, own):
        at = block * side
        return (
            source_ref[3 * face] * left_ref[at : at + side]
            + source_ref[3 * face + 1] * own
            + source_ref[3 * face + 2] * right_ref[at : at + side]
        )

    def padded(line, faces, start):
        ghosts = {}
        for layer in range(3):
            ghosts[layer] = ghost(faces[0], start + 2 + layer, line(side - 3 + layer))
            ghosts[side + 3 + layer] = ghost(faces[1], start + layer, line(layer))
        return lambda n: ghosts[n] if n in ghosts else line(n - 3)

    against_first, against_second = against_masks(speed_ref)
    sweep(padded(first_line, (0, 1), 0), against_first, spread(speed_ref, 0), flux_one)
    sweep(padded(second_line, (2, 3), 5), against_second, spread(speed_ref, 1), flux_two)
    for n in range(side):
        back = side - 1 - n
        flux_turned[n * side : (n + 1) * side] = jnp.where(
            against_second, flux_two[back * side : (back + 1) * side], flux_two[n * side : (n + 1) * side]
        )
    for n in range(side):
        back = side - 1 - n
        rows = slice(n * side, (n + 1) * side)
        change = jnp.where(against_first, flux_one[back * side : (back + 1) * side], flux_one[rows])
        change = change + flux_turned[pl.ds(n, side, stride=side), :]
        moved = u_ref[rows] - ratio * change
        if base_ref is not None:
            moved = 0.5 * base_ref[rows] + 0.5 * moved
        out_ref[rows] = moved


def spread(speed_ref, row):
    return jnp.broadcast_to(speed_ref[row : row + 1], (BSIDE, speed_ref.shape[1]))


def against_masks(speed_ref):
    return spread(speed_ref, 2) > 0.5, spread(speed_ref, 3) > 0.5


def transport_kernel(
    source_ref, ratio_ref, u_ref, speed_ref, out_ref,
    one_ref, flux_one, flux_two, flux_turned,
    strips, from_left, from_right, sent_left, sent_right, got_left, got_right,
):
    tiles = u_ref.shape[0]
    me = lax.axis_index("space")
    count = lax.axis_size("space")
    has_left, has_right = me > 0, me < count - 1
    left, right = lax.rem(me + count - 1, count), lax.rem(me + 1, count)
    mesh_ids = pl.DeviceIdType.MESH
    ratio = ratio_ref[0]
    fluxes = (flux_one, flux_two, flux_turned)

    barrier = pltpu.get_barrier_semaphore()

    @pl.when(has_left)
    def _():
        pl.semaphore_signal(barrier, inc=1, device_id={"space": left}, device_id_type=mesh_ids)

    @pl.when(has_right)
    def _():
        pl.semaphore_signal(barrier, inc=1, device_id={"space": right}, device_id_type=mesh_ids)

    pl.semaphore_wait(barrier, has_left.astype(jnp.int32) + has_right.astype(jnp.int32))

    def to_right(turn, tile):
        return pltpu.make_async_remote_copy(
            src_ref=strips.at[turn, tile], dst_ref=from_left.at[turn, tile],
            send_sem=sent_right.at[turn, tile], recv_sem=got_left.at[turn, tile],
            device_id={"space": right}, device_id_type=mesh_ids,
        )

    def to_left(turn, tile):
        return pltpu.make_async_remote_copy(
            src_ref=strips.at[turn, tile], dst_ref=from_right.at[turn, tile],
            send_sem=sent_left.at[turn, tile], recv_sem=got_right.at[turn, tile],
            device_id={"space": left}, device_id_type=mesh_ids,
        )

    def send(turn, tile, cells_ref):
        pack_strips(cells_ref.at[tile], *against_masks(speed_ref.at[tile]), strips.at[turn, tile])

        @pl.when(has_right)
        def _():
            to_right(turn, tile).start()

        @pl.when(has_left)
        def _():
            to_left(turn, tile).start()

    def receive(turn, tile):
        @pl.when(has_left)
        def _():
            to_right(turn, tile).wait_recv()

        @pl.when(has_right)
        def _():
            to_left(turn, tile).wait_recv()

    def begin(tile, carry):
        send(0, tile, u_ref)
        return carry

    lax.fori_loop(0, tiles, begin, 0)

    @pl.when(me == 0)
    def _():
        from_left[...] = jnp.zeros_like(from_left)

    @pl.when(me == count - 1)
    def _():
        from_right[...] = jnp.zeros_like(from_right)

    def first(tile, carry):
        receive(0, tile)
        advance(
            source_ref, ratio, u_ref.at[tile], None, from_left.at[0, tile], from_right.at[0, tile],
            speed_ref.at[tile], one_ref.at[tile], fluxes,
        )
        send(1, tile, one_ref)
        return carry

    lax.fori_loop(0, tiles, first, 0)

    def second(tile, carry):
        receive(1, tile)
        advance(
            source_ref, ratio, one_ref.at[tile], u_ref.at[tile], from_left.at[1, tile], from_right.at[1, tile],
            speed_ref.at[tile], out_ref.at[tile], fluxes,
        )
        return carry

    lax.fori_loop(0, tiles, second, 0)

    def finish(tile, carry):
        for turn in range(2):

            @pl.when(has_right)
            def _():
                to_right(turn, tile).wait_send()

            @pl.when(has_left)
            def _():
                to_left(turn, tile).wait_send()

        return carry

    lax.fori_loop(0, tiles, finish, 0)


def transport(source, ratio, cells, speeds):
    tiles, count, lanes = cells.shape
    smem = pl.BlockSpec(memory_space=pltpu.SMEM)
    vmem = pl.BlockSpec(memory_space=pltpu.VMEM)
    strips = pltpu.VMEM((2, tiles, 10 * BSIDE, lanes), jnp.float32)
    return pl.pallas_call(
        transport_kernel,
        in_specs=[smem, smem, vmem, vmem],
        out_specs=vmem,
        out_shape=jax.ShapeDtypeStruct(cells.shape, jnp.float32),
        scratch_shapes=[pltpu.VMEM(cells.shape, jnp.float32)]
        + [pltpu.VMEM((count, lanes), jnp.float32)] * 3
        + [strips] * 3
        + [pltpu.SemaphoreType.DMA((2, tiles))] * 4,
        compiler_params=pltpu.CompilerParams(
            collective_id=0, has_side_effects=True, vmem_limit_bytes=48 * 1024 * 1024
        ),
    )(source, ratio, cells, speeds)


def tiled(rows):
    count, width = rows.shape
    tiles = pl.cdiv(width, LANES)
    rows = jnp.pad(rows, ((0, 0), (0, tiles * LANES - width)))
    return rows.reshape(count, tiles, LANES).transpose(1, 0, 2)


def lane_pieces(tiles, width):
    return [(t, t * LANES, min(width, (t + 1) * LANES)) for t in range(tiles)]


def gather_kernel(chosen_ref, cells_ref, out_ref, picked_ref, rows_ref):
    parts, planes, each, plane = out_ref.shape
    tiles = cells_ref.shape[0]

    def one(slot, carry):
        row = chosen_ref[slot]
        for tile in range(tiles):
            picked_ref[tile, pl.ds(slot, 1), :] = cells_ref[tile, pl.ds(row, 1), :]
        return carry

    lax.fori_loop(0, parts * each, one, 0, unroll=8)
    for tile in range(tiles):
        rows_ref[:, tile * LANES : (tile + 1) * LANES] = picked_ref[tile]
    for part in range(parts):
        for n in range(planes):
            out_ref[part, n] = rows_ref[part * each : (part + 1) * each, n * plane : (n + 1) * plane]


def gather(chosen, cells, shape):
    return pl.pallas_call(
        gather_kernel,
        in_specs=[pl.BlockSpec(memory_space=pltpu.SMEM), pl.BlockSpec(memory_space=pltpu.VMEM)],
        out_specs=pl.BlockSpec(memory_space=pltpu.VMEM),
        out_shape=jax.ShapeDtypeStruct(shape, jnp.float32),
        scratch_shapes=[
            pltpu.VMEM((cells.shape[0], shape[0] * shape[2], LANES), jnp.float32),
            pltpu.VMEM((shape[0] * shape[2], cells.shape[0] * LANES), jnp.float32),
        ],
    )(chosen, cells)


def scatter_kernel(chosen_ref, count_ref, cells_ref, change_ref, out_ref, rows_ref):
    parts, planes, each, plane = change_ref.shape
    for tile, begin, end in lane_pieces(cells_ref.shape[0], out_ref.shape[1]):
        out_ref[:, begin:end] = cells_ref[tile, :, : end - begin]
    for part in range(parts):
        for n in range(planes):
            rows_ref[part * each : (part + 1) * each, n * plane : (n + 1) * plane] = change_ref[part, n]

    def one(slot, carry):
        row = pl.ds(chosen_ref[slot], 1)
        out_ref[row, :] += rows_ref[pl.ds(slot, 1), :]
        return carry

    lax.fori_loop(0, count_ref[0], one, 0)


def scatter(chosen, count, cells, change):
    smem = pl.BlockSpec(memory_space=pltpu.SMEM)
    vmem = pl.BlockSpec(memory_space=pltpu.VMEM)
    parts, planes, each, plane = change.shape
    return pl.pallas_call(
        scatter_kernel,
        in_specs=[smem, smem, vmem, vmem],
        out_specs=vmem,
        out_shape=jax.ShapeDtypeStruct((cells.shape[1], planes * plane), jnp.float32),
        scratch_shapes=[pltpu.VMEM((parts * each, planes * plane), jnp.float32)],
    )(chosen, count, cells, change)


def halves(table):
    high = table.astype(jnp.bfloat16)
    low = (table - high.astype(jnp.float32)).astype(jnp.bfloat16)
    return high, low


def dot(left, right):
    return jnp.dot(left, right, preferred_element_type=jnp.float32)


def collision(values, tables, depth):
    first_ref, second_ref, loss_ref, plane_ref, line_ref = tables
    size, plane = values.shape
    group = size // depth

    def transforms(cubes):
        high, low = halves(jnp.concatenate(cubes, axis=0) if len(cubes) > 1 else cubes[0])
        rows = high.shape[0]
        wide = dot(jnp.concatenate([high, low], axis=0), plane_ref[0])
        mapped = wide[:rows] + (wide[rows:] + dot(high, plane_ref[1]))
        results = []
        for n in range(len(cubes)):
            high, low = halves(mapped[n * size : (n + 1) * size])
            wide = dot(line_ref[...], high)
            results.append(wide[:size] + (wide[size:] + dot(line_ref[:size], low)))
        return results

    spectrum = transforms([values])[0].reshape(depth, group, plane)

    def scaled(multiplier):
        return (spectrum * multiplier[:, None, :]).reshape(size, plane)

    total = -values * transforms([scaled(loss_ref[...])])[0]

    def one(term, total):
        image_one, image_two = transforms([scaled(first_ref[term]), scaled(second_ref[term])])
        return total + image_one * image_two

    return lax.fori_loop(0, first_ref.shape[0], one, total)


def collide_kernel(cells_ref, *refs):
    depth, group, plane = cells_ref.shape
    out_ref = refs[-1]
    total = collision(cells_ref[...].reshape(depth * group, plane), refs[:-1], depth)
    out_ref[...] = total.reshape(depth, group, plane)


def swap_collide_kernel(
    cells_ref, first_ref, second_ref, loss_ref, plane_ref, line_ref, out_ref,
    first_cube, second_cube, loss_cube,
    got, result, sent_in, got_in, own_in, sent_out, got_out, own_out,
):
    parts = lax.axis_size("vel")
    blocks, planes, group, plane = cells_ref.shape
    chunks = blocks // parts
    me = lax.axis_index("vel")
    mesh_ids = pl.DeviceIdType.MESH
    peers = [lax.rem(me + n, parts) for n in range(parts)]
    tables = (first_cube, second_cube, loss_cube, plane_ref, line_ref)

    barrier = pltpu.get_barrier_semaphore()
    for peer in peers[1:]:
        pl.semaphore_signal(barrier, inc=1, device_id={"vel": peer}, device_id_type=mesh_ids)
    pl.semaphore_wait(barrier, parts - 1)

    def swap(chunk, from_ref, to_ref, send_sem, recv_sem, own_sem):
        mine = chunk * parts + me
        copies = []
        for n, peer in enumerate(peers):
            source = from_ref.at[chunk * parts + peer]
            if n == 0:
                copies.append(pltpu.make_async_copy(source, to_ref.at[mine], own_sem.at[chunk]))
            else:
                copies.append(
                    pltpu.make_async_remote_copy(
                        src_ref=source, dst_ref=to_ref.at[mine],
                        send_sem=send_sem.at[chunk, n], recv_sem=recv_sem.at[chunk, n],
                        device_id={"vel": peer}, device_id_type=mesh_ids,
                    )
                )
            copies[-1].start()
        return copies

    incoming = [swap(chunk, cells_ref, got, sent_in, got_in, own_in) for chunk in range(chunks)]
    for row in range(parts * planes):
        columns = slice(row * plane, (row + 1) * plane)
        for term in range(first_ref.shape[0]):
            first_cube[term, row : row + 1, :] = first_ref[term : term + 1, columns]
            second_cube[term, row : row + 1, :] = second_ref[term : term + 1, columns]
        loss_cube[row : row + 1, :] = loss_ref[:, columns]
    outgoing = []
    for chunk in range(chunks):
        for copy in incoming[chunk][1:]:
            copy.wait_recv()
        incoming[chunk][0].wait()
        held = slice(chunk * parts, (chunk + 1) * parts)
        values = got[held].reshape(parts * planes * group, plane)
        result[held] = collision(values, tables, parts * planes).reshape(parts, planes, group, plane)
        outgoing.append(swap(chunk, result, out_ref, sent_out, got_out, own_out))
    for copies in outgoing:
        copies[0].wait()
        for copy in copies[1:]:
            copy.wait_recv()
    for copies in incoming + outgoing:
        for copy in copies[1:]:
            copy.wait_send()


def hartley_tables(vdim):
    index = np.arange(vdim, dtype=np.float64)
    angle = 2.0 * np.pi * np.outer(index, index) / vdim
    table = (np.cos(angle) + np.sin(angle)) / np.sqrt(vdim)

    def split(wide):
        wide = wide.astype(np.float32)
        high = wide.astype(jnp.bfloat16)
        return np.stack([high, (wide - high.astype(np.float32)).astype(jnp.bfloat16)])

    return split(np.kron(table, table)), np.concatenate(split(np.kron(table, np.eye(GROUP))))


def collision_operands(gain_first, gain_second, loss_rates):
    plane_table, line_table = hartley_tables(VDIM)
    return gain_first, gain_second, loss_rates[None], jnp.asarray(plane_table), jnp.asarray(line_table)


def collide(cells, operands):
    depth, count, plane = cells.shape
    gain_first, gain_second, loss_rates = operands[:3]
    cube = (gain_first.shape[0], depth, plane)
    operands = (gain_first.reshape(cube), gain_second.reshape(cube), loss_rates.reshape(cube[1:])) + operands[3:]
    spare = -count % GROUP
    if spare:
        cells = jnp.pad(cells, ((0, 0), (0, spare), (0, 0)))
    cell_spec = pl.BlockSpec((depth, GROUP, plane), lambda n: (0, n, 0))

    def whole(shape):
        return pl.BlockSpec(shape, lambda n: (0,) * len(shape))

    result = pl.pallas_call(
        collide_kernel,
        grid=((count + spare) // GROUP,),
        in_specs=[cell_spec] + [whole(array.shape) for array in operands],
        out_specs=cell_spec,
        out_shape=jax.ShapeDtypeStruct(cells.shape, jnp.float32),
        compiler_params=pltpu.CompilerParams(vmem_limit_bytes=56 * 1024 * 1024),
    )(cells, *operands)
    return result[:, :count]


def swap_collide(cells, operands):
    chunks, parts = cells.shape[0] // lax.axis_size("vel"), lax.axis_size("vel")
    vmem = pl.BlockSpec(memory_space=pltpu.VMEM)
    across = pltpu.SemaphoreType.DMA((chunks, parts))
    own = pltpu.SemaphoreType.DMA((chunks,))
    cube = (VDIM, cells.shape[3])
    gains = pltpu.VMEM((operands[0].shape[0],) + cube, jnp.float32)
    return pl.pallas_call(
        swap_collide_kernel,
        in_specs=[vmem] * (1 + len(operands)),
        out_specs=vmem,
        out_shape=jax.ShapeDtypeStruct(cells.shape, jnp.float32),
        scratch_shapes=[gains, gains, pltpu.VMEM(cube, jnp.float32)]
        + [pltpu.VMEM(cells.shape, jnp.float32)] * 2
        + [across, across, own] * 2,
        compiler_params=pltpu.CompilerParams(
            collective_id=1, has_side_effects=True, vmem_limit_bytes=56 * 1024 * 1024
        ),
    )(cells, *operands)


def shards(
    distribution, neighbours, block_level, collide_mask, gain_first, gain_second, loss_rates
):
    blocks, cell_count, width = distribution.shape
    assert blocks == 1
    density = distribution.reshape(cell_count, width)
    speeds = speed_rows(lax.axis_index("vel") * width, width)
    ratio = courant * jnp.exp2(block_level.astype(jnp.float32))
    offset = neighbours[0] - (lax.axis_index("space") - 1)
    source = (offset[:, None] == jnp.arange(3)) & (neighbours[0] >= 0)[:, None]
    source = source.astype(jnp.float32).reshape(-1)

    section_two = transport(source, ratio, tiled(density), tiled(speeds))

    parts = lax.axis_size("vel")
    each = ACT // parts
    cell_index = jnp.arange(cell_count)
    rank = jnp.sum(jnp.where(cell_index[:, None] < cell_index, collide_mask[:, None], 0), axis=0)
    hit = (rank[:, None] == jnp.arange(ACT)) & (collide_mask > 0)[:, None]
    chosen = jnp.sum(jnp.where(hit, cell_index[:, None], 0), axis=0)
    held = jnp.sum(collide_mask)[None]

    plane = VDIM * VDIM
    operands = collision_operands(gain_first, gain_second, loss_rates)
    if width % plane == 0 and each % GROUP == 0:
        sent = gather(chosen, section_two, (ACT // GROUP, width // plane, GROUP, plane))
        change = swap_collide(sent, operands)
    else:
        sent = gather(chosen, section_two, (parts, 1, each, width))
        got = lax.all_to_all(sent, "vel", split_axis=0, concat_axis=0, tiled=True)
        got = jnp.transpose(got.reshape(parts, each, width), (1, 0, 2))
        got = got.reshape(each, VDIM, plane).transpose(1, 0, 2)
        change = collide(got, operands).transpose(1, 0, 2).reshape(each, parts, width)
        change = change.transpose(1, 0, 2)[:, None]
        change = lax.all_to_all(change, "vel", split_axis=0, concat_axis=0, tiled=True)
    return scatter(chosen, held, section_two, change).reshape(blocks, cell_count, width)


def solution(mesh):
    in_specs = (P("space", None, "vel"), P("space", None), P("space"), P("space"), P(), P(), P())
    out_specs = P("space", None, "vel")
    return jax.shard_map(shards, mesh=mesh, in_specs=in_specs, out_specs=out_specs, check_vma=False)
```
